32 devices in a mesh: row: 4 (over x, core), col: 8 (over z, y).
Axes of the slice: x: 2, y: 2, z: 4, core: 2. Of those that a mesh axis runs over, the one named last changes fastest.
Arguments:
- features: bfloat16 [8192, 256], P(('col', 'row')), may hold values from -6 to 6
- weight: bfloat16 [256, 256], replicated, may hold values from -0.375 to 0.375
- grad_out: bfloat16 [8192, 256], P(('row', 'col')), may hold values from -6 to 6
- adj_values: bfloat16 [384, 1024, 128], P('row', 'col'), may hold values from -0.15625 to 0.15625
- block_pos: int32 [4, 768], P('row', 'col'), may hold values from 0 to 127, as said below
- block_count: int32 [4, 8], P('row', 'col'), may hold values from 24 to 96, as said below
Outputs:
- activation: bfloat16 [8192, 256], P(('row', 'col'))
- grad_input: bfloat16 [8192, 256], P(('col', 'row'))
- grad_weight: float32 [256, 256], replicated
The draws below stay inside these ranges and needn't reach their ends.
Inputs may be any that keep to these rules, and one draw needn't show every extreme that they name: `block_pos`: within one tile the block positions of all 96 slots are distinct values below 128. `block_count`: some tile has exactly 96 live slots and some tile exactly 24.
All inputs are finite; a program needn't handle non-finite values.
Results may differ from the reference program's by a relative error of at most 0.018.
Values may be sent and summed in bfloat16 or wider, within the bound.
A program may use at most 128 MiB of HBM per device.

```python
import jax
import jax.numpy as jnp
from jax import lax

PB = 2
BS = 128
F = 256
N = 8192
RB = 16
CB = 8
NB_MAX = 96
N_ROW = 4
N_COL = 8


def draw_block_pos(key, part):
    tiles = N_ROW * N_COL
    total = PB * PB * N_ROW * N_COL
    tile_keys = jax.random.split(key, tiles)
    chosen = jax.vmap(lambda single: jax.random.permutation(single, total)[:NB_MAX])(tile_keys)
    return chosen.astype(jnp.int32).reshape(N_ROW, N_COL * NB_MAX)


def draw_block_count(key, part):
    tiles = N_ROW * N_COL
    counts = jax.random.randint(key, (tiles,), NB_MAX // 4, NB_MAX + 1).astype(jnp.int32)
    chosen_tile = jax.random.randint(jax.random.fold_in(key, 7), (), 0, tiles)
    counts = counts.at[chosen_tile].set(NB_MAX)
    other_tile = (chosen_tile + 1) % tiles
    counts = counts.at[other_tile].set(NB_MAX // 4)
    return counts.reshape(N_ROW, N_COL)


def shard_levels(own_key, dims, pieces, least, high):
    factor_of = 1.0
    for position, parts in pieces:
        steps = jax.random.uniform(jax.random.fold_in(jax.random.fold_in(own_key, 6), position), (parts,), jnp.float32, least / len(pieces), high / len(pieces))
        factor_of = factor_of * jnp.repeat(jnp.exp(steps), dims[position] // parts).reshape((-1,) + (1,) * (len(dims) - 1 - position))
    return factor_of


def gaussian(key, dims, scale, limit, cuts=(), kind=jnp.bfloat16):
    level = shard_levels(key, dims, cuts, -0.22, 0.18) if cuts else 1.0
    result = jax.random.normal(key, dims, jnp.float32) * scale * level
    return jnp.minimum(jnp.maximum(result, -limit), limit).astype(kind)


def setup_inputs(seed: int = 0) -> dict:
    splits = jax.random.split(jax.random.key(seed), 7)
    features = gaussian(splits[0], (N, F), 1.0, 6.0, ((0, 32),))
    weight = gaussian(splits[1], (F, F), F ** -0.5, 0.375)
    grad_out = gaussian(splits[2], (N, F), 1.0, 6.0, ((0, 32),))
    adj_values = gaussian(splits[3], (N_ROW * NB_MAX, N_COL * BS, BS), ((10 * NB_MAX * BS // RB) ** -0.5), 0.15625, ((0, 4), (1, 8)))
    block_pos = draw_block_pos(jax.random.fold_in(splits[6], 71), 0)
    block_count = draw_block_count(jax.random.fold_in(splits[6], 71), 0)
    return {"features": features, "weight": weight, "grad_out": grad_out, "adj_values": adj_values, "block_pos": block_pos, "block_count": block_count}


def tile_forward(values, positions, live_count, panel, row_blocks, col_blocks):
    slots = values.shape[0]
    block_size = values.shape[1]
    width = panel.shape[1]
    groups = 6
    per_group = slots // groups
    brow = positions // col_blocks
    bcol = positions % col_blocks
    live = (jnp.arange(slots, dtype=jnp.int32) < live_count).astype(jnp.float32)
    blocks = panel.reshape(col_blocks, block_size, width)

    def step(totals, items):
        vals, rows_idx, cols_idx, alive = items
        picked = blocks[cols_idx].astype(jnp.float32)
        prod = jnp.einsum("kij,kjf->kif", vals.astype(jnp.float32), picked)
        onehot = (rows_idx[None, :] == jnp.arange(row_blocks, dtype=jnp.int32)[:, None]).astype(jnp.float32) * alive[None, :]
        return totals + jnp.einsum("bk,kif->bif", onehot, prod), None

    items = (values.reshape(groups, per_group, block_size, block_size), brow.reshape(groups, per_group), bcol.reshape(groups, per_group), live.reshape(groups, per_group))
    start = jnp.zeros((row_blocks, block_size, width), jnp.float32)
    totals, unused = lax.scan(step, start, items)
    return totals.reshape(row_blocks * block_size, width)


def tile_backward(values, positions, live_count, grads, row_blocks, col_blocks):
    slots = values.shape[0]
    block_size = values.shape[1]
    width = grads.shape[1]
    groups = 6
    per_group = slots // groups
    brow = positions // col_blocks
    bcol = positions % col_blocks
    live = (jnp.arange(slots, dtype=jnp.int32) < live_count).astype(jnp.float32)
    blocks = grads.reshape(row_blocks, block_size, width)

    def step(totals, items):
        vals, rows_idx, cols_idx, alive = items
        picked = blocks[rows_idx].astype(jnp.float32)
        prod = jnp.einsum("kij,kif->kjf", vals.astype(jnp.float32), picked)
        onehot = (cols_idx[None, :] == jnp.arange(col_blocks, dtype=jnp.int32)[:, None]).astype(jnp.float32) * alive[None, :]
        return totals + jnp.einsum("bk,kjf->bjf", onehot, prod), None

    items = (values.reshape(groups, per_group, block_size, block_size), brow.reshape(groups, per_group), bcol.reshape(groups, per_group), live.reshape(groups, per_group))
    start = jnp.zeros((col_blocks, block_size, width), jnp.float32)
    totals, unused = lax.scan(step, start, items)
    return totals.reshape(col_blocks * block_size, width)


def round_part(part):
    rounded = lax.optimization_barrier(part.astype(jnp.bfloat16))
    return rounded.astype(jnp.float32)


def reference(features, weight, grad_out, adj_values, block_pos, block_count):
    rows_tile = RB * BS
    cols_tile = CB * BS
    xw = jnp.dot(features, weight, preferred_element_type=jnp.float32).astype(jnp.bfloat16)
    positions_all = block_pos.reshape(N_ROW, N_COL, NB_MAX)
    value_rows = adj_values.reshape(N_ROW, NB_MAX, N_COL * BS, BS)

    def forward_row(index_row):
        tile_vals = value_rows[index_row]

        def over_cols(totals, index_col):
            vals = lax.dynamic_slice_in_dim(tile_vals, index_col * BS, BS, 1)
            panel = lax.dynamic_slice_in_dim(xw, index_col * cols_tile, cols_tile, 0)
            part = tile_forward(vals, positions_all[index_row, index_col], block_count[index_row, index_col], panel, RB, CB)
            return totals + round_part(part), None

        totals, unused = lax.scan(over_cols, jnp.zeros((rows_tile, F), jnp.float32), jnp.arange(N_COL, dtype=jnp.int32))
        return totals

    hidden = lax.map(forward_row, jnp.arange(N_ROW, dtype=jnp.int32)).reshape(N, F)
    sigma = jax.nn.sigmoid(hidden)
    activation = (hidden * sigma).astype(jnp.bfloat16)
    grad_hidden = (grad_out.astype(jnp.float32) * sigma * (1.0 + hidden * (1.0 - sigma))).astype(jnp.bfloat16)

    def backward_col(index_col):
        def over_rows(totals, index_row):
            vals = lax.dynamic_slice_in_dim(value_rows[index_row], index_col * BS, BS, 1)
            grads = lax.dynamic_slice_in_dim(grad_hidden, index_row * rows_tile, rows_tile, 0)
            part = tile_backward(vals, positions_all[index_row, index_col], block_count[index_row, index_col], grads, RB, CB)
            return totals + round_part(part), None

        totals, unused = lax.scan(over_rows, jnp.zeros((cols_tile, F), jnp.float32), jnp.arange(N_ROW, dtype=jnp.int32))
        return totals

    grad_xw = lax.map(backward_col, jnp.arange(N_COL, dtype=jnp.int32)).reshape(N, F).astype(jnp.bfloat16)
    grad_weight = lax.dot_general(features, grad_xw, (((0,), (0,)), ((), ())), preferred_element_type=jnp.float32)
    grad_input = lax.dot_general(grad_xw, weight, (((1,), (1,)), ((), ())), preferred_element_type=jnp.float32).astype(jnp.bfloat16)
    return activation, grad_input, grad_weight
```

```python
import functools

import jax
import jax.numpy as jnp
from jax import lax
from jax.experimental import pallas as pl
from jax.experimental.pallas import tpu as pltpu
from jax.sharding import PartitionSpec as P

MESH = pl.DeviceIdType.MESH
F32 = jnp.float32
BF16 = jnp.bfloat16


def split_axis(size, inner):
    while size % inner:
        inner -= 1
    return size // inner, inner


def kernel(
    dims,
    inv_ref,
    feat_ref,
    weight_ref,
    gout_ref,
    adj_ref,
    act_ref,
    gin_ref,
    gw_ref,
    vals,
    dense,
    dense_t,
    feats,
    feats_t,
    xw,
    wbuf,
    gout,
    cs_y,
    cr_y,
    cs_z,
    cr_z,
    ghs,
    acc,
    rs_y,
    rr_y,
    rs_z,
    rr_z,
    ws,
    wr,
    w2,
    w3,
    local_sem,
    sem_f,
    sem_fr,
    sem_cy,
    sem_cz,
    sem_g,
    sem_gr,
    sem_ry,
    sem_rz,
    sem_w1,
    sem_w2,
    sem_w2r,
    sem_w3,
    sem_w3r,
):
    (nrow, ncol, ro, ri, co, ci) = dims
    slots, bs, _ = adj_ref.shape
    own, width = feat_ref.shape
    row_blocks = dense.shape[0] // bs
    col_blocks = dense.shape[1] // bs
    row = lax.axis_index("row")
    col = lax.axis_index("col")
    rx, rc = lax.div(row, ri), lax.rem(row, ri)
    cz, cy = lax.div(col, ci), lax.rem(col, ci)

    def remote(src, dst, send, recv, axis, peer):
        return pltpu.make_async_remote_copy(
            src_ref=src,
            dst_ref=dst,
            send_sem=send,
            recv_sem=recv,
            device_id={axis: peer},
            device_id_type=MESH,
        )

    loads = [
        pltpu.make_async_copy(feat_ref, feats.at[row], local_sem.at[0]),
        pltpu.make_async_copy(weight_ref, wbuf, local_sem.at[1]),
        pltpu.make_async_copy(adj_ref, vals.at[pl.ds(0, slots)], local_sem.at[2]),
        pltpu.make_async_copy(gout_ref, gout, local_sem.at[3]),
    ]
    for load in loads:
        load.start()

    barrier = pltpu.get_barrier_semaphore()
    for d in range(1, nrow):
        pl.semaphore_signal(
            barrier, inc=1, device_id={"row": lax.rem(row + d, nrow)}, device_id_type=MESH
        )
    for d in range(1, ncol):
        pl.semaphore_signal(
            barrier, inc=1, device_id={"col": lax.rem(col + d, ncol)}, device_id_type=MESH
        )
    vals[slots] = jnp.zeros((bs, bs), vals.dtype)
    loads[0].wait()
    pl.semaphore_wait(barrier, nrow + ncol - 2)

    def gather(axis, buf, outer, inner, n_out, n_in, send, recv, hook):
        me = outer * n_in + inner
        started = []
        slot = 0

        def push(block, peer):
            copy = remote(
                buf.at[block], buf.at[block], send.at[len(started)], recv.at[block], axis, peer
            )
            copy.start()
            started.append(copy)

        def arrive(block):
            remote(buf.at[block], buf.at[block], send.at[0], recv.at[block], axis, me).wait_recv()

        for d in range(n_out - 1, 0, -1):
            push(me, lax.rem(outer + d, n_out) * n_in + inner)
        for e in range(1, n_in):
            push(me, outer * n_in + lax.rem(inner + e, n_in))
        hook(me)
        for d in range(1, n_out):
            source = lax.rem(outer + d, n_out)
            block = source * n_in + inner
            arrive(block)
            for e in range(1, n_in):
                push(block, outer * n_in + lax.rem(inner + e, n_in))
            hook(block)
        for d in range(n_out):
            source = lax.rem(outer + d, n_out)
            for e in range(1, n_in):
                block = source * n_in + lax.rem(inner + n_in - e, n_in)
                arrive(block)
                hook(block)
        return started

    def rows(block):
        return pl.ds(pl.multiple_of(block * own, own), own)

    def project(block):
        xw[rows(block), :] = jnp.dot(
            feats[block], wbuf[...], preferred_element_type=F32
        ).astype(BF16)
        feats_t[:, rows(block)] = feats[block].T

    def first(block):
        loads[1].wait()
        loads[2].wait()

        def fill(r, carry):
            for c in range(col_blocks):
                tile = vals[inv_ref[r * col_blocks + c]]
                at = pl.ds(pl.multiple_of(r * bs, bs), bs)
                dense[at, c * bs : (c + 1) * bs] = tile
                dense_t[c * bs : (c + 1) * bs, at] = tile.T
            return carry

        lax.fori_loop(0, row_blocks, fill, 0)
        project(block)

    calls = [first]

    def feature_hook(block):
        (calls.pop() if calls else project)(block)

    pending = gather("row", feats, rx, rc, ro, ri, sem_f, sem_fr, feature_hook)

    def reduce_start(axis, part, outer, inner, n_out, n_in, s_in, r_in, sems):
        copies = []
        for d in list(range(1, n_out)) + [0]:
            to = lax.rem(outer + d, n_out)
            for e in range(1, n_in):
                peer = lax.rem(inner + e, n_in)
                slot = d * (n_in - 1) + e - 1
                s_in[slot] = part(to * n_in + peer).astype(BF16)
                copy = remote(
                    s_in.at[slot],
                    r_in.at[to * (n_in - 1) + e - 1],
                    sems.at[0, slot],
                    sems.at[1, to * (n_in - 1) + e - 1],
                    axis,
                    outer * n_in + peer,
                )
                copy.start()
                copies.append(copy)
        return copies

    def reduce_middle(axis, part, outer, inner, n_out, n_in, r_in, s_out, r_out, sem_i, sem_o):
        copies = []
        total = None
        for d in list(range(1, n_out)) + [0]:
            to = lax.rem(outer + d, n_out)
            value = part(to * n_in + inner)
            for e in range(1, n_in):
                at = to * (n_in - 1) + e - 1
                remote(
                    r_in.at[at], r_in.at[at], sem_i.at[0, 0], sem_i.at[1, at], axis, 0
                ).wait_recv()
                value = value + r_in[at].astype(F32)
            if d == 0:
                total = value
            else:
                s_out[d - 1] = value.astype(BF16)
                copy = remote(
                    s_out.at[d - 1],
                    r_out.at[d - 1],
                    sem_o.at[0, d - 1],
                    sem_o.at[1, d - 1],
                    axis,
                    to * n_in + inner,
                )
                copy.start()
                copies.append(copy)
        return copies, total

    def reduce_end(total, copies, r_out):
        for d, copy in enumerate(copies):
            copy.wait_recv()
            total = total + r_out[d].astype(F32)
        return total

    def forward(block):
        return jnp.dot(dense[rows(block), :], xw[...], preferred_element_type=F32)

    pending += reduce_start("col", forward, cz, cy, co, ci, cs_y, cr_y, sem_cy)
    copies, total = reduce_middle(
        "col", forward, cz, cy, co, ci, cr_y, cs_z, cr_z, sem_cy, sem_cz
    )
    hidden = reduce_end(total, copies, cr_z)
    pending += copies
    loads[3].wait()
    sigma = jax.nn.sigmoid(hidden)
    ghs[col] = (gout[...].astype(F32) * sigma * (1.0 + hidden * (1.0 - sigma))).astype(BF16)
    act_ref[...] = (hidden * sigma).astype(BF16)

    seen = []

    def backward(block):
        term = jnp.dot(dense_t[:, rows(block)], ghs[block], preferred_element_type=F32)
        acc[...] = acc[...] + term if seen else term
        seen.append(1)

    pending += gather("col", ghs, cz, cy, co, ci, sem_g, sem_gr, backward)

    grad = jnp.dot(feats_t[...], acc[...].astype(BF16), preferred_element_type=F32)
    part_rows = width // ncol
    ws[...] = grad.astype(BF16).reshape(ncol, part_rows, width)
    w1 = []
    for d in range(1, ncol):
        peer = lax.rem(col + d, ncol)
        copy = remote(
            ws.at[peer], wr.at[d - 1], sem_w1.at[0, d - 1], sem_w1.at[1, d - 1], "col", peer
        )
        copy.start()
        w1.append(copy)

    def back(block):
        return acc[rows(block), :]

    pending += reduce_start("row", back, rx, rc, ro, ri, rs_y, rr_y, sem_ry)
    copies, total = reduce_middle(
        "row", back, rx, rc, ro, ri, rr_y, rs_z, rr_z, sem_ry, sem_rz
    )
    pending += copies

    share = ws[col].astype(F32)
    for d, copy in enumerate(w1):
        copy.wait_recv()
        share = share + wr[d].astype(F32)
    w2[row] = share.astype(BF16)
    w2_copies = []
    for d in range(1, nrow):
        copy = remote(
            w2.at[row], w2.at[row], sem_w2.at[d - 1], sem_w2r.at[row], "row", lax.rem(row + d, nrow)
        )
        copy.start()
        w2_copies.append(copy)

    grad_xw = reduce_end(total, copies, rr_z).astype(BF16)
    gin_ref[...] = lax.dot_general(
        grad_xw, wbuf[...], (((1,), (1,)), ((), ())), preferred_element_type=F32
    ).astype(BF16)

    for d in range(1, nrow):
        source = lax.rem(row + d, nrow)
        remote(
            w2.at[source], w2.at[source], sem_w2.at[0], sem_w2r.at[source], "row", source
        ).wait_recv()
    share = w2[0].astype(F32)
    for d in range(1, nrow):
        share = share + w2[d].astype(F32)
    w3[col] = share.astype(BF16)
    w3_copies = []
    for d in range(1, ncol):
        copy = remote(
            w3.at[col], w3.at[col], sem_w3.at[d - 1], sem_w3r.at[col], "col", lax.rem(col + d, ncol)
        )
        copy.start()
        w3_copies.append(copy)
    for d in range(1, ncol):
        source = lax.rem(col + d, ncol)
        remote(
            w3.at[source], w3.at[source], sem_w3.at[0], sem_w3r.at[source], "col", source
        ).wait_recv()
    gw_ref[...] = w3[...].astype(F32).reshape(width, width)
    for copy in pending + w1 + w2_copies + w3_copies:
        copy.wait_send()


def solution(mesh):
    nrow, ncol = mesh.shape["row"], mesh.shape["col"]
    ro, ri = split_axis(nrow, 2)
    zs = 4 if ncol % 4 == 0 else 1
    co, ci = zs, ncol // zs
    dims = (nrow, ncol, ro, ri, co, ci)

    def body(features, weight, grad_out, adj_values, block_pos, block_count):
        own, width = features.shape
        slots, bs, _ = adj_values.shape
        rows_tile = own * ncol
        cols_tile = own * nrow
        spots = (rows_tile // bs) * (cols_tile // bs)
        order = jnp.arange(slots, dtype=jnp.int32)
        hit = (block_pos[0][None, :] == jnp.arange(spots, dtype=jnp.int32)[:, None]) & (
            order < block_count[0, 0]
        )[None, :]
        inv = slots + jnp.sum(jnp.where(hit, order - slots, 0), axis=1)
        block = lambda n: pltpu.VMEM((max(n, 1), own, width), BF16)
        dma = pltpu.SemaphoreType.DMA
        part_rows = width // ncol

        def ag_sends(o, i):
            return max((o - 1) + (i - 1) + (o - 1) * (i - 1), 1)

        scratch = [
            pltpu.VMEM((slots + 1, bs, bs), BF16),
            pltpu.VMEM((rows_tile, cols_tile), BF16),
            pltpu.VMEM((cols_tile, rows_tile), BF16),
            block(nrow),
            pltpu.VMEM((width, cols_tile), BF16),
            pltpu.VMEM((cols_tile, width), BF16),
            pltpu.VMEM((width, width), BF16),
            pltpu.VMEM((own, width), BF16),
            block(co * (ci - 1)),
            block(co * (ci - 1)),
            block(co - 1),
            block(co - 1),
            block(ncol),
            pltpu.VMEM((cols_tile, width), F32),
            block(ro * (ri - 1)),
            block(ro * (ri - 1)),
            block(ro - 1),
            block(ro - 1),
            pltpu.VMEM((ncol, part_rows, width), BF16),
            pltpu.VMEM((ncol, part_rows, width), BF16),
            pltpu.VMEM((nrow, part_rows, width), BF16),
            pltpu.VMEM((ncol, part_rows, width), BF16),
            dma((4,)),
            dma((ag_sends(ro, ri),)),
            dma((nrow,)),
            dma((2, max(co * (ci - 1), 1))),
            dma((2, max(co - 1, 1))),
            dma((ag_sends(co, ci),)),
            dma((ncol,)),
            dma((2, max(ro * (ri - 1), 1))),
            dma((2, max(ro - 1, 1))),
            dma((2, ncol)),
            dma((nrow,)),
            dma((nrow,)),
            dma((ncol,)),
            dma((ncol,)),
        ]
        anyspace = pl.BlockSpec(memory_space=pl.ANY)
        return pl.pallas_call(
            functools.partial(kernel, dims),
            out_shape=(
                jax.ShapeDtypeStruct((own, width), BF16),
                jax.ShapeDtypeStruct((own, width), BF16),
                jax.ShapeDtypeStruct((width, width), F32),
            ),
            in_specs=[pl.BlockSpec(memory_space=pltpu.SMEM)] + [anyspace] * 4,
            out_specs=[pl.BlockSpec(memory_space=pltpu.VMEM)] * 3,
            scratch_shapes=scratch,
            compiler_params=pltpu.CompilerParams(
                collective_id=0,
                has_side_effects=True,
                vmem_limit_bytes=66 * 1000 * 1000,
            ),
        )(inv, features, weight, grad_out, adj_values)

    placed = (
        P(("col", "row"), None),
        P(),
        P(("row", "col"), None),
        P("row", "col", None),
        P("row", "col"),
        P("row", "col"),
    )
    return jax.shard_map(
        body,
        mesh=mesh,
        in_specs=placed,
        out_specs=(P(("row", "col"), None), P(("col", "row"), None), P()),
        check_vma=False,
    )
```

```python
import functools

import jax
import jax.numpy as jnp
from jax import lax
from jax.experimental import pallas as pl
from jax.experimental.pallas import tpu as pltpu
from jax.sharding import PartitionSpec as P

MESH = pl.DeviceIdType.MESH
F32 = jnp.float32
BF16 = jnp.bfloat16


def split_axis(size, inner):
    while size % inner:
        inner -= 1
    return size // inner, inner


class Reduce:
    def __init__(self, link, axis, outer, inner, n_out, n_in, part, bufs, sems):
        self.link, self.axis, self.part = link, axis, part
        self.outer, self.inner, self.n_out, self.n_in = outer, inner, n_out, n_in
        self.s_in, self.r_in, self.s_out, self.r_out = bufs
        self.sem_in, self.sem_out = sems
        self.sent, self.totals = [], {}

    def to(self, d):
        return lax.rem(self.outer + d, self.n_out)

    def start(self, h, d):
        to = self.to(d)
        for e in range(1, self.n_in):
            peer = lax.rem(self.inner + e, self.n_in)
            slot = (h * self.n_out + d) * (self.n_in - 1) + e - 1
            there = (h * self.n_out + to) * (self.n_in - 1) + e - 1
            self.s_in[slot] = self.part(to * self.n_in + peer, h).astype(BF16)
            copy = self.link(
                self.s_in.at[slot],
                self.r_in.at[there],
                self.sem_in.at[0, slot],
                self.sem_in.at[1, there],
                self.axis,
                self.outer * self.n_in + peer,
            )
            copy.start()
            self.sent.append(copy)

    def middle(self, h, d):
        to = self.to(d)
        value = self.part(to * self.n_in + self.inner, h)
        for e in range(1, self.n_in):
            at = (h * self.n_out + to) * (self.n_in - 1) + e - 1
            self.link(
                self.r_in.at[at],
                self.r_in.at[at],
                self.sem_in.at[0, 0],
                self.sem_in.at[1, at],
                self.axis,
                0,
            ).wait_recv()
            value = value + self.r_in[at].astype(F32)
        if d == 0:
            self.totals[h] = value
            return
        slot = h * (self.n_out - 1) + d - 1
        self.s_out[slot] = value.astype(BF16)
        copy = self.link(
            self.s_out.at[slot],
            self.r_out.at[slot],
            self.sem_out.at[0, slot],
            self.sem_out.at[1, slot],
            self.axis,
            to * self.n_in + self.inner,
        )
        copy.start()
        self.sent.append(copy)

    def end(self, h):
        total = self.totals[h]
        for d in range(1, self.n_out):
            slot = h * (self.n_out - 1) + d - 1
            self.link(
                self.r_out.at[slot],
                self.r_out.at[slot],
                self.sem_out.at[0, slot],
                self.sem_out.at[1, slot],
                self.axis,
                0,
            ).wait_recv()
            total = total + self.r_out[slot].astype(F32)
        return total


class Gather:
    def __init__(self, link, axis, outer, inner, n_out, n_in, halves, buf, send, recv):
        self.link, self.axis, self.halves = link, axis, halves
        self.outer, self.inner, self.n_out, self.n_in = outer, inner, n_out, n_in
        self.buf, self.send, self.recv = buf, send, recv
        self.me = outer * n_in + inner
        self.sent = []

    def push(self, block, h, peer):
        at = block * self.halves + h
        copy = self.link(
            self.buf.at[at],
            self.buf.at[at],
            self.send.at[len(self.sent)],
            self.recv.at[at],
            self.axis,
            peer,
        )
        copy.start()
        self.sent.append(copy)

    def arrive(self, block, h):
        at = block * self.halves + h
        self.link(
            self.buf.at[at], self.buf.at[at], self.send.at[0], self.recv.at[at], self.axis, 0
        ).wait_recv()

    def forward(self, block, h):
        for e in range(1, self.n_in):
            self.push(block, h, self.outer * self.n_in + lax.rem(self.inner + e, self.n_in))

    def start(self, h):
        for d in range(self.n_out - 1, 0, -1):
            self.push(self.me, h, lax.rem(self.outer + d, self.n_out) * self.n_in + self.inner)
        self.forward(self.me, h)

    def from_outer(self, h, d):
        block = lax.rem(self.outer + d, self.n_out) * self.n_in + self.inner
        self.arrive(block, h)
        self.forward(block, h)
        return [block]

    def from_inner(self, h, d):
        blocks = []
        for e in range(1, self.n_in):
            block = lax.rem(self.outer + d, self.n_out) * self.n_in + lax.rem(
                self.inner + e, self.n_in
            )
            self.arrive(block, h)
            blocks.append(block)
        return blocks


def kernel(
    dims,
    count_ref,
    pos_ref,
    feat_ref,
    weight_ref,
    gout_ref,
    adj_ref,
    act_ref,
    gin_ref,
    gw_ref,
    inv_v,
    inv_s,
    vals,
    dense,
    dense_t,
    feats,
    wbuf,
    gout,
    cs_y,
    cr_y,
    cs_z,
    cr_z,
    af,
    ghs,
    acc,
    rs_y,
    rr_y,
    rs_z,
    rr_z,
    ws1,
    wr1,
    ws2,
    wr2,
    w4,
    local_sem,
    sem_f,
    sem_fr,
    sem_cy,
    sem_cz,
    sem_g,
    sem_gr,
    sem_ry,
    sem_rz,
    sem_w1,
    sem_w2,
    sem_w3,
    sem_w3r,
    sem_w4,
    sem_w4r,
):
    (nrow, ncol, ro, ri, co, ci, halves) = dims
    slots, bs, _ = adj_ref.shape
    own, width = feat_ref.shape
    half = own // halves
    row_blocks = dense.shape[0] // bs
    col_blocks = dense.shape[1] // bs
    spots = row_blocks * col_blocks
    row = lax.axis_index("row")
    col = lax.axis_index("col")
    rx, rc = lax.div(row, ri), lax.rem(row, ri)
    cz, cy = lax.div(col, ci), lax.rem(col, ci)

    def remote(src, dst, send, recv, axis, peer):
        return pltpu.make_async_remote_copy(
            src_ref=src,
            dst_ref=dst,
            send_sem=send,
            recv_sem=recv,
            device_id={axis: peer},
            device_id_type=MESH,
        )

    loads = [
        pltpu.make_async_copy(feat_ref, feats.at[row], local_sem.at[0]),
        pltpu.make_async_copy(adj_ref, vals.at[pl.ds(0, slots)], local_sem.at[1]),
        pltpu.make_async_copy(weight_ref, wbuf, local_sem.at[2]),
        pltpu.make_async_copy(gout_ref, gout, local_sem.at[3]),
    ]
    for load in loads:
        load.start()

    barrier = pltpu.get_barrier_semaphore()
    for d in range(1, nrow):
        pl.semaphore_signal(
            barrier, inc=1, device_id={"row": lax.rem(row + d, nrow)}, device_id_type=MESH
        )
    for d in range(1, ncol):
        pl.semaphore_signal(
            barrier, inc=1, device_id={"col": lax.rem(col + d, ncol)}, device_id_type=MESH
        )
    slot = lax.broadcasted_iota(jnp.int32, (spots, slots), 1)
    spot = lax.broadcasted_iota(jnp.int32, (spots, slots), 0)
    hit = (pos_ref[...] == spot) & (slot < count_ref[0, 0])
    found = slots + jnp.sum(jnp.where(hit, slot - slots, 0), axis=1, keepdims=True)
    inv_v[...] = jnp.broadcast_to(found, (spots, 128)).T[:8]
    table = pltpu.make_async_copy(inv_v, inv_s, local_sem.at[4])
    table.start()
    vals[slots] = jnp.zeros((bs, bs), vals.dtype)
    loads[0].wait()
    pl.semaphore_wait(barrier, nrow + ncol - 2)

    g1 = Gather(remote, "row", rx, rc, ro, ri, 1, feats, sem_f, sem_fr)
    g1.start(0)
    table.wait()
    loads[1].wait()

    def fill(r, carry):
        for c in range(col_blocks):
            tile = vals[inv_s[0, r * col_blocks + c]]
            at = pl.ds(pl.multiple_of(r * bs, bs), bs)
            dense[at, c * bs : (c + 1) * bs] = tile
            dense_t[c * bs : (c + 1) * bs, at] = tile.T
        return carry

    lax.fori_loop(0, row_blocks, fill, 0)
    for d in range(1, ro):
        g1.from_outer(0, d)
    for d in range(ro):
        g1.from_inner(0, d)

    def rows(block, h=0, size=own):
        return pl.ds(pl.multiple_of(block * own + h * size, size), size)

    def forward(block, h):
        return jnp.dot(
            dense[rows(block, h, half), :],
            feats[...].reshape(nrow * own, width),
            preferred_element_type=F32,
        )

    rsc = Reduce(
        remote, "col", cz, cy, co, ci, forward, (cs_y, cr_y, cs_z, cr_z), (sem_cy, sem_cz)
    )
    agc = Gather(remote, "col", cz, cy, co, ci, halves, ghs, sem_g, sem_gr)
    order = list(range(1, co)) + [0]
    for h in range(halves):
        for d in order:
            rsc.start(h, d)
    loads[2].wait()
    loads[3].wait()

    def owner(h):
        piece = rsc.end(h).astype(BF16)
        at = slice(h * half, (h + 1) * half)
        af[at, :] = piece
        hidden = jnp.dot(piece, wbuf[...], preferred_element_type=F32)
        sigma = jax.nn.sigmoid(hidden)
        ghs[col * halves + h] = (
            gout[at, :].astype(F32) * sigma * (1.0 + hidden * (1.0 - sigma))
        ).astype(BF16)
        agc.start(h)
        act_ref[at, :] = (hidden * sigma).astype(BF16)

    for d in order:
        rsc.middle(0, d)
    for h in range(1, halves):
        for d in order[:-1]:
            rsc.middle(h, d)
        owner(h - 1)
        rsc.middle(h, 0)
    owner(halves - 1)

    grad = jnp.dot(
        af[...].T,
        ghs[pl.ds(col * halves, halves)].reshape(own, width),
        preferred_element_type=F32,
    )
    rows1 = width // nrow
    rows2 = rows1 // ncol
    ws1[...] = grad.astype(BF16).reshape(nrow, rows1, width)
    w1 = []
    for d in range(1, nrow):
        peer = lax.rem(row + d, nrow)
        copy = remote(
            ws1.at[peer], wr1.at[d - 1], sem_w1.at[0, d - 1], sem_w1.at[1, d - 1], "row", peer
        )
        copy.start()
        w1.append(copy)

    seen = []

    def backward(blocks):
        for block in blocks:
            term = jnp.dot(
                dense_t[:, rows(block)],
                ghs[pl.ds(block * halves, halves)].reshape(own, width),
                preferred_element_type=F32,
            )
            acc[...] = acc[...] + term if seen else term
            seen.append(1)

    last = halves - 1
    for h in range(last):
        for d in range(1, co):
            agc.from_outer(h, d)
    backward([agc.me])

    share = ws1[row].astype(F32)
    for d, copy in enumerate(w1):
        copy.wait_recv()
        share = share + wr1[d].astype(F32)
    for k in range(ncol):
        ws2[k] = share[k * rows2 : (k + 1) * rows2].astype(BF16)
    w2 = []
    for d in range(1, ncol):
        peer = lax.rem(col + d, ncol)
        copy = remote(
            ws2.at[peer], wr2.at[d - 1], sem_w2.at[0, d - 1], sem_w2.at[1, d - 1], "col", peer
        )
        copy.start()
        w2.append(copy)

    for d in range(1, co):
        backward(agc.from_outer(last, d))
    for h in range(last):
        for d in range(co):
            agc.from_inner(h, d)

    share = ws2[col].astype(F32)
    for d, copy in enumerate(w2):
        copy.wait_recv()
        share = share + wr2[d].astype(F32)
    w4[row, col] = share.astype(BF16)
    w3 = []
    for d in range(1, ncol):
        peer = lax.rem(col + d, ncol)
        copy = remote(
            w4.at[row, col], w4.at[row, col], sem_w3.at[d - 1], sem_w3r.at[col], "col", peer
        )
        copy.start()
        w3.append(copy)

    for d in range(co):
        backward(agc.from_inner(last, d))

    def back(block, h):
        return acc[rows(block), :]

    rsr = Reduce(
        remote, "row", rx, rc, ro, ri, back, (rs_y, rr_y, rs_z, rr_z), (sem_ry, sem_rz)
    )
    order = list(range(1, ro)) + [0]
    for d in order:
        rsr.start(0, d)

    for d in range(1, ncol):
        source = lax.rem(col + d, ncol)
        remote(
            w4.at[row, source], w4.at[row, source], sem_w3.at[0], sem_w3r.at[source], "col", source
        ).wait_recv()
    w4c = []
    for d in range(1, nrow):
        peer = lax.rem(row + d, nrow)
        copy = remote(w4.at[row], w4.at[row], sem_w4.at[d - 1], sem_w4r.at[row], "row", peer)
        copy.start()
        w4c.append(copy)

    for d in order:
        rsr.middle(0, d)
    for d in range(1, nrow):
        source = lax.rem(row + d, nrow)
        remote(
            w4.at[source], w4.at[source], sem_w4.at[0], sem_w4r.at[source], "row", source
        ).wait_recv()
    for r in range(nrow):
        for k in range(ncol):
            at = r * rows1 + k * rows2
            gw_ref[at : at + rows2, :] = w4[r, k].astype(F32)
    gin_ref[...] = lax.dot_general(
        rsr.end(0).astype(BF16), wbuf[...], (((1,), (1,)), ((), ())), preferred_element_type=F32
    ).astype(BF16)
    for copy in g1.sent + rsc.sent + agc.sent + rsr.sent + w1 + w2 + w3 + w4c:
        copy.wait_send()


def hand_on(a_in, b_in, c_in, a_out, b_out, c_out):
    a_out[...] = a_in[...]
    b_out[...] = b_in[...]
    c_out[...] = c_in[...]


def solution(mesh):
    nrow, ncol = mesh.shape["row"], mesh.shape["col"]
    ro, ri = split_axis(nrow, 2)
    co = 4 if ncol % 4 == 0 else 1
    ci = ncol // co
    halves = 2
    dims = (nrow, ncol, ro, ri, co, ci, halves)

    def body(features, weight, grad_out, adj_values, block_pos, block_count):
        own, width = features.shape
        slots, bs, _ = adj_values.shape
        rows_tile = own * ncol
        cols_tile = own * nrow
        spots = (rows_tile // bs) * (cols_tile // bs)
        half = own // halves
        rows1 = width // nrow
        rows2 = rows1 // ncol
        dma = pltpu.SemaphoreType.DMA

        def block(n, rows):
            return pltpu.VMEM((max(n, 1), rows, width), BF16)

        def ag_sends(o, i):
            return max((o - 1) + (i - 1) + (o - 1) * (i - 1), 1)

        scratch = [
            pltpu.VMEM((8, spots), jnp.int32),
            pltpu.SMEM((8, spots), jnp.int32),
            pltpu.VMEM((slots + 1, bs, bs), BF16),
            pltpu.VMEM((rows_tile, cols_tile), BF16),
            pltpu.VMEM((cols_tile, rows_tile), BF16),
            block(nrow, own),
            pltpu.VMEM((width, width), BF16),
            pltpu.VMEM((own, width), BF16),
            block(halves * co * (ci - 1), half),
            block(halves * co * (ci - 1), half),
            block(halves * (co - 1), half),
            block(halves * (co - 1), half),
            pltpu.VMEM((own, width), BF16),
            block(ncol * halves, half),
            pltpu.VMEM((cols_tile, width), F32),
            block(ro * (ri - 1), own),
            block(ro * (ri - 1), own),
            block(ro - 1, own),
            block(ro - 1, own),
            block(nrow, rows1),
            block(nrow - 1, rows1),
            block(ncol, rows2),
            block(ncol - 1, rows2),
            pltpu.VMEM((nrow, ncol, rows2, width), BF16),
            dma((5,)),
            dma((ag_sends(ro, ri),)),
            dma((nrow,)),
            dma((2, max(halves * co * (ci - 1), 1))),
            dma((2, max(halves * (co - 1), 1))),
            dma((halves * ag_sends(co, ci),)),
            dma((halves * ncol,)),
            dma((2, max(ro * (ri - 1), 1))),
            dma((2, max(ro - 1, 1))),
            dma((2, nrow)),
            dma((2, ncol)),
            dma((ncol,)),
            dma((ncol,)),
            dma((nrow,)),
            dma((nrow,)),
        ]
        anyspace = pl.BlockSpec(memory_space=pl.ANY)
        vmem = pl.BlockSpec(memory_space=pltpu.VMEM)
        shapes = (
            jax.ShapeDtypeStruct((own, width), BF16),
            jax.ShapeDtypeStruct((own, width), BF16),
            jax.ShapeDtypeStruct((width, width), F32),
        )
        outs = pl.pallas_call(
            functools.partial(kernel, dims),
            out_shape=shapes,
            in_specs=[pl.BlockSpec(memory_space=pltpu.SMEM), vmem] + [anyspace] * 4,
            out_specs=[vmem] * 3,
            scratch_shapes=scratch,
            compiler_params=pltpu.CompilerParams(
                collective_id=0,
                has_side_effects=True,
                vmem_limit_bytes=66 * 1000 * 1000,
            ),
        )(block_count, block_pos, features, weight, grad_out, adj_values)
        return pl.pallas_call(
            hand_on, out_shape=shapes, in_specs=[vmem] * 3, out_specs=[vmem] * 3
        )(*outs)

    placed = (
        P(("col", "row"), None),
        P(),
        P(("row", "col"), None),
        P("row", "col", None),
        P("row", "col"),
        P("row", "col"),
    )
    return jax.shard_map(
        body,
        mesh=mesh,
        in_specs=placed,
        out_specs=(P(("row", "col"), None), P(("col", "row"), None), P()),
        check_vma=False,
    )
```

```python
import functools

import jax
import jax.numpy as jnp
from jax import lax
from jax.experimental import pallas as pl
from jax.experimental.pallas import tpu as pltpu
from jax.sharding import PartitionSpec as P

MESH = pl.DeviceIdType.MESH
F32 = jnp.float32
BF16 = jnp.bfloat16


def split_axis(size, inner):
    while size % inner:
        inner -= 1
    return size // inner, inner


class Reduce:
    def __init__(self, link, axis, outer, inner, n_out, n_in, part, bufs, sems):
        self.link, self.axis, self.part = link, axis, part
        self.outer, self.inner, self.n_out, self.n_in = outer, inner, n_out, n_in
        self.s_in, self.r_in, self.s_out, self.r_out = bufs
        self.sem_in, self.sem_out = sems
        self.sent, self.totals, self.held, self.line = [], {}, {}, None

    def to(self, d):
        return lax.rem(self.outer + d, self.n_out)

    def start(self, h, d):
        to = self.to(d)
        for e in range(1, self.n_in):
            peer = lax.rem(self.inner + e, self.n_in)
            slot = (h * self.n_out + d) * (self.n_in - 1) + e - 1
            there = (h * self.n_out + to) * (self.n_in - 1) + e - 1
            self.s_in[slot] = self.part(to * self.n_in + peer, h).astype(BF16)
            copy = self.link(
                self.s_in.at[slot],
                self.r_in.at[there],
                self.sem_in.at[0, slot],
                self.sem_in.at[1, there],
                self.axis,
                self.outer * self.n_in + peer,
            )
            copy.start()
            self.sent.append(copy)

    def middle(self, h, d):
        to = self.to(d)
        value = self.part(to * self.n_in + self.inner, h)
        for e in range(1, self.n_in):
            at = (h * self.n_out + to) * (self.n_in - 1) + e - 1
            self.link(
                self.r_in.at[at],
                self.r_in.at[at],
                self.sem_in.at[0, 0],
                self.sem_in.at[1, at],
                self.axis,
                0,
            ).wait_recv()
            value = value + self.r_in[at].astype(F32)
        if d == 0:
            self.totals[h] = value
            return
        slot = h * (self.n_out - 1) + d - 1
        self.s_out[slot] = value.astype(BF16)
        copy = self.link(
            self.s_out.at[slot],
            self.r_out.at[slot],
            self.sem_out.at[0, slot],
            self.sem_out.at[1, slot],
            self.axis,
            to * self.n_in + self.inner,
        )
        copy.start()
        self.sent.append(copy)

    def end(self, h):
        total = self.totals[h]
        for d in range(1, self.n_out):
            slot = h * (self.n_out - 1) + d - 1
            self.link(
                self.r_out.at[slot],
                self.r_out.at[slot],
                self.sem_out.at[0, slot],
                self.sem_out.at[1, slot],
                self.axis,
                0,
            ).wait_recv()
            total = total + self.r_out[slot].astype(F32)
        return total


class Gather:
    def __init__(self, link, axis, outer, inner, n_out, n_in, halves, buf, send, recv):
        self.link, self.axis, self.halves = link, axis, halves
        self.outer, self.inner, self.n_out, self.n_in = outer, inner, n_out, n_in
        self.buf, self.send, self.recv = buf, send, recv
        self.me = outer * n_in + inner
        self.sent, self.maybe, self.slots, self.line = [], [], 0, None

    def push(self, block, h, peer):
        at = block * self.halves + h
        copy = self.link(
            self.buf.at[at],
            self.buf.at[at],
            self.send.at[len(self.sent) + self.slots],
            self.recv.at[at],
            self.axis,
            peer,
        )
        copy.start()
        self.sent.append(copy)

    def arrive(self, block, h):
        at = block * self.halves + h
        self.link(
            self.buf.at[at], self.buf.at[at], self.send.at[0], self.recv.at[at], self.axis, 0
        ).wait_recv()

    def forward(self, block, h):
        for e in range(1, self.n_in):
            self.push(block, h, self.outer * self.n_in + lax.rem(self.inner + e, self.n_in))

    def start(self, h):
        for d in range(self.n_out - 1, 0, -1):
            self.push(self.me, h, lax.rem(self.outer + d, self.n_out) * self.n_in + self.inner)
        self.forward(self.me, h)

    def from_outer(self, h, d):
        block = lax.rem(self.outer + d, self.n_out) * self.n_in + self.inner
        self.arrive(block, h)
        self.forward(block, h)
        return [block]

    def from_inner(self, h, d):
        blocks = []
        for e in range(1, self.n_in):
            block = lax.rem(self.outer + d, self.n_out) * self.n_in + lax.rem(
                self.inner + e, self.n_in
            )
            self.arrive(block, h)
            blocks.append(block)
        return blocks


class Line:
    def __init__(self, at):
        self.central = lax.rem(lax.div(at + 1, 2), 2) == 1
        self.mate = at + 1 - 2 * lax.rem(at, 2)
        self.near = 2 - lax.div(at, 2)
        self.place = (at, self.mate, self.near, 3 * (self.near - 1))


class TreeReduce(Reduce):
    def to(self, d):
        return self.line.place[d]

    def hop(self, h, d, peer, landing):
        slot = h * 4 + d
        copy = self.link(
            self.s_out.at[slot],
            self.r_out.at[h * 4 + landing],
            self.sem_out.at[0, slot],
            self.sem_out.at[1, h * 4 + landing],
            self.axis,
            peer * self.n_in + self.inner,
        )
        copy.start()
        self.sent.append(copy)

    def landed(self, h, slot):
        at = h * 4 + slot
        self.link(
            self.r_out.at[at],
            self.r_out.at[at],
            self.sem_out.at[0, at],
            self.sem_out.at[1, at],
            self.axis,
            0,
        ).wait_recv()
        return self.r_out[at].astype(F32)

    def middle(self, h, d):
        value = self.part(self.to(d) * self.n_in + self.inner, h)
        for e in range(1, self.n_in):
            at = (h * self.n_out + self.to(d)) * (self.n_in - 1) + e - 1
            self.link(
                self.r_in.at[at],
                self.r_in.at[at],
                self.sem_in.at[0, 0],
                self.sem_in.at[1, at],
                self.axis,
                0,
            ).wait_recv()
            value = value + self.r_in[at].astype(F32)
        line = self.line
        if d == 0:
            self.totals[h] = value
        elif d == 1:
            self.s_out[h * 4 + d] = value.astype(BF16)
            self.hop(h, d, line.mate, 0)
        else:
            self.s_out[h * 4 + d] = value.astype(BF16)
            rim = jnp.logical_not(line.central)

            @pl.when(rim)
            def _():
                self.hop(h, d, line.mate, d)

            self.sent.pop()
            self.held[h, d] = value

    def join(self, h, d):
        line = self.line

        @pl.when(line.central)
        def _():
            total = self.held[h, d] + self.landed(h, d)
            self.s_out[h * 4 + d] = total.astype(BF16)
            self.hop(h, d, line.place[d], 1)

        self.sent.pop()
        slot = h * 4 + d
        self.sent.append(
            self.link(
                self.s_out.at[slot],
                self.s_out.at[slot],
                self.sem_out.at[0, slot],
                self.sem_out.at[1, slot],
                self.axis,
                0,
            )
        )

    def end(self, h):
        return self.totals[h] + self.landed(h, 0) + self.landed(h, 1)


class TreeGather(Gather):
    def start(self, h):
        self.push(self.me, h, self.line.near * self.n_in + self.inner)
        self.push(self.me, h, self.line.mate * self.n_in + self.inner)
        self.forward(self.me, h)

    def from_outer(self, h, d):
        block = self.line.place[d] * self.n_in + self.inner
        self.arrive(block, h)
        if d > 1:

            @pl.when(self.line.central)
            def _():
                self.push(block, h, self.line.mate * self.n_in + self.inner)

            self.sent.pop()
            at = self.me * self.halves + h
            self.maybe.append(
                self.link(
                    self.buf.at[at],
                    self.buf.at[at],
                    self.send.at[len(self.sent) + self.slots],
                    self.recv.at[at],
                    self.axis,
                    0,
                )
            )
            self.slots += 1
        self.forward(block, h)
        return [block]

    def from_inner(self, h, d):
        blocks = []
        for e in range(1, self.n_in):
            block = self.line.place[d] * self.n_in + lax.rem(self.inner + e, self.n_in)
            self.arrive(block, h)
            blocks.append(block)
        return blocks


def kernel(
    dims,
    count_ref,
    pos_ref,
    feat_ref,
    weight_ref,
    gout_ref,
    adj_ref,
    act_ref,
    gin_ref,
    gw_ref,
    inv_v,
    inv_s,
    vals,
    dense,
    dense_t,
    feats,
    wbuf,
    gout,
    cs_y,
    cr_y,
    cs_z,
    cr_z,
    af,
    ghs,
    acc,
    rs_y,
    rr_y,
    rs_z,
    rr_z,
    ws1,
    wr1,
    ws2,
    wr2,
    w4,
    local_sem,
    sem_f,
    sem_fr,
    sem_cy,
    sem_cz,
    sem_g,
    sem_gr,
    sem_ry,
    sem_rz,
    sem_w1,
    sem_w2,
    sem_w3,
    sem_w3r,
    sem_w4,
    sem_w4r,
):
    (nrow, ncol, ro, ri, co, ci, halves) = dims
    slots, bs, _ = adj_ref.shape
    own, width = feat_ref.shape
    half = own // halves
    row_blocks = dense.shape[0] // bs
    col_blocks = dense.shape[1] // bs
    spots = row_blocks * col_blocks
    row = lax.axis_index("row")
    col = lax.axis_index("col")
    rx, rc = lax.div(row, ri), lax.rem(row, ri)
    cz, cy = lax.div(col, ci), lax.rem(col, ci)

    def remote(src, dst, send, recv, axis, peer):
        return pltpu.make_async_remote_copy(
            src_ref=src,
            dst_ref=dst,
            send_sem=send,
            recv_sem=recv,
            device_id={axis: peer},
            device_id_type=MESH,
        )

    loads = [
        pltpu.make_async_copy(feat_ref, feats.at[row], local_sem.at[0]),
        pltpu.make_async_copy(adj_ref, vals.at[pl.ds(0, slots)], local_sem.at[1]),
        pltpu.make_async_copy(weight_ref, wbuf, local_sem.at[2]),
        pltpu.make_async_copy(gout_ref, gout, local_sem.at[3]),
    ]
    for load in loads:
        load.start()

    barrier = pltpu.get_barrier_semaphore()
    for d in range(1, nrow):
        pl.semaphore_signal(
            barrier, inc=1, device_id={"row": lax.rem(row + d, nrow)}, device_id_type=MESH
        )
    for d in range(1, ncol):
        pl.semaphore_signal(
            barrier, inc=1, device_id={"col": lax.rem(col + d, ncol)}, device_id_type=MESH
        )
    slot = lax.broadcasted_iota(jnp.int32, (spots, slots), 1)
    spot = lax.broadcasted_iota(jnp.int32, (spots, slots), 0)
    hit = (pos_ref[...] == spot) & (slot < count_ref[0, 0])
    found = slots + jnp.sum(jnp.where(hit, slot - slots, 0), axis=1, keepdims=True)
    inv_v[...] = jnp.broadcast_to(found, (spots, 128)).T[:8]
    table = pltpu.make_async_copy(inv_v, inv_s, local_sem.at[4])
    table.start()
    vals[slots] = jnp.zeros((bs, bs), vals.dtype)
    loads[0].wait()
    pl.semaphore_wait(barrier, nrow + ncol - 2)

    g1 = Gather(remote, "row", rx, rc, ro, ri, 1, feats, sem_f, sem_fr)
    g1.start(0)
    table.wait()
    loads[1].wait()

    def fill(r, carry):
        for c in range(col_blocks):
            tile = vals[inv_s[0, r * col_blocks + c]]
            at = pl.ds(pl.multiple_of(r * bs, bs), bs)
            dense[at, c * bs : (c + 1) * bs] = tile
            dense_t[c * bs : (c + 1) * bs, at] = tile.T
        return carry

    lax.fori_loop(0, row_blocks, fill, 0)
    for d in range(1, ro):
        g1.from_outer(0, d)
    for d in range(ro):
        g1.from_inner(0, d)

    def rows(block, h=0, size=own):
        return pl.ds(pl.multiple_of(block * own + h * size, size), size)

    def forward(block, h):
        return jnp.dot(
            dense[rows(block, h, half), :],
            feats[...].reshape(nrow * own, width),
            preferred_element_type=F32,
        )

    line = Line(cz)
    rsc = TreeReduce(
        remote, "col", cz, cy, co, ci, forward, (cs_y, cr_y, cs_z, cr_z), (sem_cy, sem_cz)
    )
    agc = TreeGather(remote, "col", cz, cy, co, ci, halves, ghs, sem_g, sem_gr)
    rsc.line = agc.line = line
    order = [2, 3, 1, 0]
    for h in range(halves):
        for d in order:
            rsc.start(h, d)
    loads[2].wait()
    loads[3].wait()

    def owner(h):
        piece = rsc.end(h).astype(BF16)
        at = slice(h * half, (h + 1) * half)
        af[at, :] = piece
        hidden = jnp.dot(piece, wbuf[...], preferred_element_type=F32)
        sigma = jax.nn.sigmoid(hidden)
        ghs[col * halves + h] = (
            gout[at, :].astype(F32) * sigma * (1.0 + hidden * (1.0 - sigma))
        ).astype(BF16)
        agc.start(h)
        act_ref[at, :] = (hidden * sigma).astype(BF16)

    for h in range(halves):
        for d in order[:-1]:
            rsc.middle(h, d)
        if h:
            owner(h - 1)
        rsc.join(h, 2)
        rsc.join(h, 3)
        rsc.middle(h, 0)
    owner(halves - 1)

    grad = jnp.dot(
        af[...].T,
        ghs[pl.ds(col * halves, halves)].reshape(own, width),
        preferred_element_type=F32,
    )
    rows1 = width // nrow
    rows2 = rows1 // ncol
    ws1[...] = grad.astype(BF16).reshape(nrow, rows1, width)
    w1 = []
    for d in range(1, nrow):
        peer = lax.rem(row + d, nrow)
        copy = remote(
            ws1.at[peer], wr1.at[d - 1], sem_w1.at[0, d - 1], sem_w1.at[1, d - 1], "row", peer
        )
        copy.start()
        w1.append(copy)

    seen = []

    def backward(blocks):
        for block in blocks:
            term = jnp.dot(
                dense_t[:, rows(block)],
                ghs[pl.ds(block * halves, halves)].reshape(own, width),
                preferred_element_type=F32,
            )
            acc[...] = acc[...] + term if seen else term
            seen.append(1)

    last = halves - 1
    for h in range(last):
        for d in range(1, co):
            agc.from_outer(h, d)
    backward([agc.me])

    share = ws1[row].astype(F32)
    for d, copy in enumerate(w1):
        copy.wait_recv()
        share = share + wr1[d].astype(F32)
    for k in range(ncol):
        ws2[k] = share[k * rows2 : (k + 1) * rows2].astype(BF16)
    w2 = []
    for d in range(1, ncol):
        peer = lax.rem(col + d, ncol)
        copy = remote(
            ws2.at[peer], wr2.at[d - 1], sem_w2.at[0, d - 1], sem_w2.at[1, d - 1], "col", peer
        )
        copy.start()
        w2.append(copy)

    for d in range(1, co):
        backward(agc.from_outer(last, d))
    for h in range(last):
        for d in range(co):
            agc.from_inner(h, d)

    share = ws2[col].astype(F32)
    for d, copy in enumerate(w2):
        copy.wait_recv()
        share = share + wr2[d].astype(F32)
    w4[row, col] = share.astype(BF16)
    w3 = []
    for d in range(1, ncol):
        peer = lax.rem(col + d, ncol)
        copy = remote(
            w4.at[row, col], w4.at[row, col], sem_w3.at[d - 1], sem_w3r.at[col], "col", peer
        )
        copy.start()
        w3.append(copy)

    for d in range(co):
        backward(agc.from_inner(last, d))

    def back(block, h):
        return acc[rows(block), :]

    rsr = Reduce(
        remote, "row", rx, rc, ro, ri, back, (rs_y, rr_y, rs_z, rr_z), (sem_ry, sem_rz)
    )
    order = list(range(1, ro)) + [0]
    for d in order:
        rsr.start(0, d)

    for d in range(1, ncol):
        source = lax.rem(col + d, ncol)
        remote(
            w4.at[row, source], w4.at[row, source], sem_w3.at[0], sem_w3r.at[source], "col", source
        ).wait_recv()
    w4c = []
    for d in range(1, nrow):
        peer = lax.rem(row + d, nrow)
        copy = remote(w4.at[row], w4.at[row], sem_w4.at[d - 1], sem_w4r.at[row], "row", peer)
        copy.start()
        w4c.append(copy)

    for d in order:
        rsr.middle(0, d)
    for d in range(1, nrow):
        source = lax.rem(row + d, nrow)
        remote(
            w4.at[source], w4.at[source], sem_w4.at[0], sem_w4r.at[source], "row", source
        ).wait_recv()
    for r in range(nrow):
        for k in range(ncol):
            at = r * rows1 + k * rows2
            gw_ref[at : at + rows2, :] = w4[r, k].astype(F32)
    gin_ref[...] = lax.dot_general(
        rsr.end(0).astype(BF16), wbuf[...], (((1,), (1,)), ((), ())), preferred_element_type=F32
    ).astype(BF16)
    @pl.when(line.central)
    def _():
        for copy in agc.maybe:
            copy.wait_send()

    for copy in g1.sent + rsc.sent + agc.sent + rsr.sent + w1 + w2 + w3 + w4c:
        copy.wait_send()


def hand_on(a_in, b_in, c_in, a_out, b_out, c_out):
    a_out[...] = a_in[...]
    b_out[...] = b_in[...]
    c_out[...] = c_in[...]


def solution(mesh):
    nrow, ncol = mesh.shape["row"], mesh.shape["col"]
    ro, ri = split_axis(nrow, 2)
    co = 4
    ci = ncol // co
    halves = 2
    dims = (nrow, ncol, ro, ri, co, ci, halves)

    def body(features, weight, grad_out, adj_values, block_pos, block_count):
        own, width = features.shape
        slots, bs, _ = adj_values.shape
        rows_tile = own * ncol
        cols_tile = own * nrow
        spots = (rows_tile // bs) * (cols_tile // bs)
        half = own // halves
        rows1 = width // nrow
        rows2 = rows1 // ncol
        dma = pltpu.SemaphoreType.DMA

        def block(n, rows):
            return pltpu.VMEM((max(n, 1), rows, width), BF16)

        def ag_sends(o, i):
            return max((o - 1) + (i - 1) + (o - 1) * (i - 1), 1)

        scratch = [
            pltpu.VMEM((8, spots), jnp.int32),
            pltpu.SMEM((8, spots), jnp.int32),
            pltpu.VMEM((slots + 1, bs, bs), BF16),
            pltpu.VMEM((rows_tile, cols_tile), BF16),
            pltpu.VMEM((cols_tile, rows_tile), BF16),
            block(nrow, own),
            pltpu.VMEM((width, width), BF16),
            pltpu.VMEM((own, width), BF16),
            block(halves * co * (ci - 1), half),
            block(halves * co * (ci - 1), half),
            block(halves * co, half),
            block(halves * co, half),
            pltpu.VMEM((own, width), BF16),
            block(ncol * halves, half),
            pltpu.VMEM((cols_tile, width), F32),
            block(ro * (ri - 1), own),
            block(ro * (ri - 1), own),
            block(ro - 1, own),
            block(ro - 1, own),
            block(nrow, rows1),
            block(nrow - 1, rows1),
            block(ncol, rows2),
            block(ncol - 1, rows2),
            pltpu.VMEM((nrow, ncol, rows2, width), BF16),
            dma((5,)),
            dma((ag_sends(ro, ri),)),
            dma((nrow,)),
            dma((2, max(halves * co * (ci - 1), 1))),
            dma((2, halves * co)),
            dma((halves * (ag_sends(co, ci) + 1),)),
            dma((halves * ncol,)),
            dma((2, max(ro * (ri - 1), 1))),
            dma((2, max(ro - 1, 1))),
            dma((2, nrow)),
            dma((2, ncol)),
            dma((ncol,)),
            dma((ncol,)),
            dma((nrow,)),
            dma((nrow,)),
        ]
        anyspace = pl.BlockSpec(memory_space=pl.ANY)
        vmem = pl.BlockSpec(memory_space=pltpu.VMEM)
        shapes = (
            jax.ShapeDtypeStruct((own, width), BF16),
            jax.ShapeDtypeStruct((own, width), BF16),
            jax.ShapeDtypeStruct((width, width), F32),
        )
        outs = pl.pallas_call(
            functools.partial(kernel, dims),
            out_shape=shapes,
            in_specs=[pl.BlockSpec(memory_space=pltpu.SMEM), vmem] + [anyspace] * 4,
            out_specs=[vmem] * 3,
            scratch_shapes=scratch,
            compiler_params=pltpu.CompilerParams(
                collective_id=0,
                has_side_effects=True,
                vmem_limit_bytes=66 * 1000 * 1000,
            ),
        )(block_count, block_pos, features, weight, grad_out, adj_values)
        return pl.pallas_call(
            hand_on, out_shape=shapes, in_specs=[vmem] * 3, out_specs=[vmem] * 3
        )(*outs)

    placed = (
        P(("col", "row"), None),
        P(),
        P(("row", "col"), None),
        P("row", "col", None),
        P("row", "col"),
        P("row", "col"),
    )
    return jax.shard_map(
        body,
        mesh=mesh,
        in_specs=placed,
        out_specs=(P(("row", "col"), None), P(("col", "row"), None), P()),
        check_vma=False,
    )
```

```python
import functools

import jax
import jax.numpy as jnp
from jax import lax
from jax.experimental import pallas as pl
from jax.experimental.pallas import tpu as pltpu
from jax.sharding import PartitionSpec as P

MESH = pl.DeviceIdType.MESH
F32 = jnp.float32
BF16 = jnp.bfloat16


def split_axis(size, inner):
    while size % inner:
        inner -= 1
    return size // inner, inner


class Reduce:
    def __init__(self, link, axis, outer, inner, n_out, n_in, part, bufs, sems):
        self.link, self.axis, self.part = link, axis, part
        self.outer, self.inner, self.n_out, self.n_in = outer, inner, n_out, n_in
        self.s_in, self.r_in, self.s_out, self.r_out = bufs
        self.sem_in, self.sem_out = sems
        self.sent, self.totals, self.held, self.line = [], {}, {}, None

    def to(self, d):
        return lax.rem(self.outer + d, self.n_out)

    def start(self, h, d):
        to = self.to(d)
        for e in range(1, self.n_in):
            peer = lax.rem(self.inner + e, self.n_in)
            slot = (h * self.n_out + d) * (self.n_in - 1) + e - 1
            there = (h * self.n_out + to) * (self.n_in - 1) + e - 1
            self.s_in[slot] = self.part(to * self.n_in + peer, h).astype(BF16)
            copy = self.link(
                self.s_in.at[slot],
                self.r_in.at[there],
                self.sem_in.at[0, slot],
                self.sem_in.at[1, there],
                self.axis,
                self.outer * self.n_in + peer,
            )
            copy.start()
            self.sent.append(copy)

    def middle(self, h, d):
        to = self.to(d)
        value = self.part(to * self.n_in + self.inner, h)
        for e in range(1, self.n_in):
            at = (h * self.n_out + to) * (self.n_in - 1) + e - 1
            self.link(
                self.r_in.at[at],
                self.r_in.at[at],
                self.sem_in.at[0, 0],
                self.sem_in.at[1, at],
                self.axis,
                0,
            ).wait_recv()
            value = value + self.r_in[at].astype(F32)
        if d == 0:
            self.totals[h] = value
            return
        slot = h * (self.n_out - 1) + d - 1
        self.s_out[slot] = value.astype(BF16)
        copy = self.link(
            self.s_out.at[slot],
            self.r_out.at[slot],
            self.sem_out.at[0, slot],
            self.sem_out.at[1, slot],
            self.axis,
            to * self.n_in + self.inner,
        )
        copy.start()
        self.sent.append(copy)

    def end(self, h):
        total = self.totals[h]
        for d in range(1, self.n_out):
            slot = h * (self.n_out - 1) + d - 1
            self.link(
                self.r_out.at[slot],
                self.r_out.at[slot],
                self.sem_out.at[0, slot],
                self.sem_out.at[1, slot],
                self.axis,
                0,
            ).wait_recv()
            total = total + self.r_out[slot].astype(F32)
        return total


class Gather:
    def __init__(self, link, axis, outer, inner, n_out, n_in, halves, buf, send, recv):
        self.link, self.axis, self.halves = link, axis, halves
        self.outer, self.inner, self.n_out, self.n_in = outer, inner, n_out, n_in
        self.buf, self.send, self.recv = buf, send, recv
        self.me = outer * n_in + inner
        self.sent, self.maybe, self.slots, self.line = [], [], 0, None

    def push(self, block, h, peer):
        at = block * self.halves + h
        copy = self.link(
            self.buf.at[at],
            self.buf.at[at],
            self.send.at[len(self.sent) + self.slots],
            self.recv.at[at],
            self.axis,
            peer,
        )
        copy.start()
        self.sent.append(copy)

    def arrive(self, block, h):
        at = block * self.halves + h
        self.link(
            self.buf.at[at], self.buf.at[at], self.send.at[0], self.recv.at[at], self.axis, 0
        ).wait_recv()

    def forward(self, block, h):
        for e in range(1, self.n_in):
            self.push(block, h, self.outer * self.n_in + lax.rem(self.inner + e, self.n_in))

    def start(self, h):
        for d in range(self.n_out - 1, 0, -1):
            self.push(self.me, h, lax.rem(self.outer + d, self.n_out) * self.n_in + self.inner)
        self.forward(self.me, h)

    def from_outer(self, h, d):
        block = lax.rem(self.outer + d, self.n_out) * self.n_in + self.inner
        self.arrive(block, h)
        self.forward(block, h)
        return [block]

    def from_inner(self, h, d):
        blocks = []
        for e in range(1, self.n_in):
            block = lax.rem(self.outer + d, self.n_out) * self.n_in + lax.rem(
                self.inner + e, self.n_in
            )
            self.arrive(block, h)
            blocks.append(block)
        return blocks


class Line:
    def __init__(self, at):
        self.central = lax.rem(lax.div(at + 1, 2), 2) == 1
        self.mate = at + 1 - 2 * lax.rem(at, 2)
        self.near = 2 - lax.div(at, 2)
        self.place = (at, self.mate, self.near, 3 * (self.near - 1))


class TreeReduce(Reduce):
    def to(self, d):
        return self.line.place[d]

    def hop(self, h, d, peer, landing):
        slot = h * 4 + d
        copy = self.link(
            self.s_out.at[slot],
            self.r_out.at[h * 4 + landing],
            self.sem_out.at[0, slot],
            self.sem_out.at[1, h * 4 + landing],
            self.axis,
            peer * self.n_in + self.inner,
        )
        copy.start()
        self.sent.append(copy)

    def landed(self, h, slot):
        at = h * 4 + slot
        self.link(
            self.r_out.at[at],
            self.r_out.at[at],
            self.sem_out.at[0, at],
            self.sem_out.at[1, at],
            self.axis,
            0,
        ).wait_recv()
        return self.r_out[at].astype(F32)

    def middle(self, h, d):
        value = self.part(self.to(d) * self.n_in + self.inner, h)
        for e in range(1, self.n_in):
            at = (h * self.n_out + self.to(d)) * (self.n_in - 1) + e - 1
            self.link(
                self.r_in.at[at],
                self.r_in.at[at],
                self.sem_in.at[0, 0],
                self.sem_in.at[1, at],
                self.axis,
                0,
            ).wait_recv()
            value = value + self.r_in[at].astype(F32)
        line = self.line
        if d == 0:
            self.totals[h] = value
        elif d == 1:
            self.s_out[h * 4 + d] = value.astype(BF16)
            self.hop(h, d, line.mate, 0)
        else:
            self.s_out[h * 4 + d] = value.astype(BF16)
            rim = jnp.logical_not(line.central)

            @pl.when(rim)
            def _():
                self.hop(h, d, line.mate, d)

            self.sent.pop()
            self.held[h, d] = value

    def join(self, h, d):
        line = self.line

        @pl.when(line.central)
        def _():
            total = self.held[h, d] + self.landed(h, d)
            self.s_out[h * 4 + d] = total.astype(BF16)
            self.hop(h, d, line.place[d], 1)

        self.sent.pop()
        slot = h * 4 + d
        self.sent.append(
            self.link(
                self.s_out.at[slot],
                self.s_out.at[slot],
                self.sem_out.at[0, slot],
                self.sem_out.at[1, slot],
                self.axis,
                0,
            )
        )

    def end(self, h):
        return self.totals[h] + self.landed(h, 0) + self.landed(h, 1)


class TreeGather(Gather):
    def start(self, h):
        self.push(self.me, h, self.line.near * self.n_in + self.inner)
        self.push(self.me, h, self.line.mate * self.n_in + self.inner)
        self.forward(self.me, h)

    def from_outer(self, h, d):
        block = self.line.place[d] * self.n_in + self.inner
        self.arrive(block, h)
        if d > 1:

            @pl.when(self.line.central)
            def _():
                self.push(block, h, self.line.mate * self.n_in + self.inner)

            self.sent.pop()
            at = self.me * self.halves + h
            self.maybe.append(
                self.link(
                    self.buf.at[at],
                    self.buf.at[at],
                    self.send.at[len(self.sent) + self.slots],
                    self.recv.at[at],
                    self.axis,
                    0,
                )
            )
            self.slots += 1
        self.forward(block, h)
        return [block]

    def from_inner(self, h, d):
        blocks = []
        for e in range(1, self.n_in):
            block = self.line.place[d] * self.n_in + lax.rem(self.inner + e, self.n_in)
            self.arrive(block, h)
            blocks.append(block)
        return blocks


def kernel(
    dims,
    count_ref,
    pos_ref,
    feat_ref,
    weight_ref,
    gout_ref,
    adj_ref,
    act_ref,
    gin_ref,
    gw_ref,
    inv_v,
    inv_s,
    vals,
    dense,
    dense_t,
    feats,
    wbuf,
    gout,
    cs_y,
    cr_y,
    cs_z,
    cr_z,
    af,
    ghs,
    acc,
    rs_y,
    rr_y,
    rs_z,
    rr_z,
    ws1,
    wr1,
    ws2,
    wr2,
    w4,
    local_sem,
    sem_f,
    sem_fr,
    sem_cy,
    sem_cz,
    sem_g,
    sem_gr,
    sem_ry,
    sem_rz,
    sem_w1,
    sem_w2,
    sem_w3,
    sem_w3r,
    sem_w4,
    sem_w4r,
):
    (nrow, ncol, ro, ri, co, ci, halves) = dims
    slots, bs, _ = adj_ref.shape
    own, width = feat_ref.shape
    half = own // halves
    row_blocks = dense.shape[0] // bs
    col_blocks = dense.shape[1] // bs
    spots = row_blocks * col_blocks
    row = lax.axis_index("row")
    col = lax.axis_index("col")
    rx, rc = lax.div(row, ri), lax.rem(row, ri)
    cz, cy = lax.div(col, ci), lax.rem(col, ci)

    def remote(src, dst, send, recv, axis, peer):
        return pltpu.make_async_remote_copy(
            src_ref=src,
            dst_ref=dst,
            send_sem=send,
            recv_sem=recv,
            device_id={axis: peer},
            device_id_type=MESH,
        )

    loads = [
        pltpu.make_async_copy(feat_ref, feats.at[row], local_sem.at[0]),
        pltpu.make_async_copy(adj_ref, vals.at[pl.ds(0, slots)], local_sem.at[1]),
        pltpu.make_async_copy(weight_ref, wbuf, local_sem.at[2]),
        pltpu.make_async_copy(gout_ref, gout, local_sem.at[3]),
    ]
    for load in loads:
        load.start()

    barrier = pltpu.get_barrier_semaphore()
    for d in range(1, nrow):
        pl.semaphore_signal(
            barrier, inc=1, device_id={"row": lax.rem(row + d, nrow)}, device_id_type=MESH
        )
    for d in range(1, ncol):
        pl.semaphore_signal(
            barrier, inc=1, device_id={"col": lax.rem(col + d, ncol)}, device_id_type=MESH
        )
    slot = lax.broadcasted_iota(jnp.int32, (spots, slots), 1)
    spot = lax.broadcasted_iota(jnp.int32, (spots, slots), 0)
    hit = (pos_ref[...] == spot) & (slot < count_ref[0, 0])
    found = slots + jnp.sum(jnp.where(hit, slot - slots, 0), axis=1, keepdims=True)
    inv_v[...] = jnp.broadcast_to(found, (spots, 128)).T[:8]
    table = pltpu.make_async_copy(inv_v, inv_s, local_sem.at[4])
    table.start()
    vals[slots] = jnp.zeros((bs, bs), vals.dtype)
    loads[0].wait()
    pl.semaphore_wait(barrier, nrow + ncol - 2)

    g1 = Gather(remote, "row", rx, rc, ro, ri, 1, feats, sem_f, sem_fr)
    g1.start(0)
    table.wait()
    loads[1].wait()

    def fill(r, carry):
        for c in range(col_blocks):
            tile = vals[inv_s[0, r * col_blocks + c]]
            at = pl.ds(pl.multiple_of(r * bs, bs), bs)
            dense[at, c * bs : (c + 1) * bs] = tile
            dense_t[c * bs : (c + 1) * bs, at] = tile.T
        return carry

    lax.fori_loop(0, row_blocks, fill, 0)
    for d in range(1, ro):
        g1.from_outer(0, d)
    for d in range(ro):
        g1.from_inner(0, d)

    def rows(block, h=0, size=own):
        return pl.ds(pl.multiple_of(block * own + h * size, size), size)

    def forward(block, h):
        return jnp.dot(
            dense[rows(block, h, half), :],
            feats[...].reshape(nrow * own, width),
            preferred_element_type=F32,
        )

    line = Line(cz)
    rsc = TreeReduce(
        remote, "col", cz, cy, co, ci, forward, (cs_y, cr_y, cs_z, cr_z), (sem_cy, sem_cz)
    )
    agc = TreeGather(remote, "col", cz, cy, co, ci, halves, ghs, sem_g, sem_gr)
    rsc.line = agc.line = line
    order = [2, 3, 1, 0]
    for h in range(halves):
        for d in order:
            rsc.start(h, d)
    loads[2].wait()
    loads[3].wait()

    def owner(h):
        piece = rsc.end(h).astype(BF16)
        at = slice(h * half, (h + 1) * half)
        af[at, :] = piece
        hidden = jnp.dot(piece, wbuf[...], preferred_element_type=F32)
        sigma = jax.nn.sigmoid(hidden)
        ghs[col * halves + h] = (
            gout[at, :].astype(F32) * sigma * (1.0 + hidden * (1.0 - sigma))
        ).astype(BF16)
        agc.start(h)
        act_ref[at, :] = (hidden * sigma).astype(BF16)

    for h in range(halves):
        for d in order[:-1]:
            rsc.middle(h, d)
        if h:
            owner(h - 1)
        rsc.join(h, 2)
        rsc.join(h, 3)
        rsc.middle(h, 0)
    owner(halves - 1)

    grad = jnp.dot(
        af[...].T,
        ghs[pl.ds(col * halves, halves)].reshape(own, width),
        preferred_element_type=F32,
    )
    rows1 = width // nrow
    rows2 = rows1 // ncol
    ws1[...] = grad.astype(BF16).reshape(nrow, rows1, width)
    w1 = []
    for d in range(1, nrow):
        peer = lax.rem(row + d, nrow)
        copy = remote(
            ws1.at[peer], wr1.at[d - 1], sem_w1.at[0, d - 1], sem_w1.at[1, d - 1], "row", peer
        )
        copy.start()
        w1.append(copy)

    seen = []

    def backward(blocks):
        for block in blocks:
            term = jnp.dot(
                dense_t[:, rows(block)],
                ghs[pl.ds(block * halves, halves)].reshape(own, width),
                preferred_element_type=F32,
            )
            acc[...] = acc[...] + term if seen else term
            seen.append(1)

    last = halves - 1
    for h in range(last):
        for d in range(1, co):
            agc.from_outer(h, d)
    backward([agc.me])

    share = ws1[row].astype(F32)
    for d, copy in enumerate(w1):
        copy.wait_recv()
        share = share + wr1[d].astype(F32)
    for k in range(ncol):
        ws2[k] = share[k * rows2 : (k + 1) * rows2].astype(BF16)
    w2 = []
    for d in range(1, ncol):
        peer = lax.rem(col + d, ncol)
        copy = remote(
            ws2.at[peer], wr2.at[d - 1], sem_w2.at[0, d - 1], sem_w2.at[1, d - 1], "col", peer
        )
        copy.start()
        w2.append(copy)

    arrived = []
    for d in range(1, co):
        arrived += agc.from_outer(last, d)
        if d > 1:
            backward([arrived.pop(0)])
    backward(arrived)

    share = ws2[col].astype(F32)
    for d, copy in enumerate(w2):
        copy.wait_recv()
        share = share + wr2[d].astype(F32)
    w4[row, col] = share.astype(BF16)
    w3 = []
    for d in range(1, ncol):
        peer = lax.rem(col + d, ncol)
        copy = remote(
            w4.at[row, col], w4.at[row, col], sem_w3.at[d - 1], sem_w3r.at[col], "col", peer
        )
        copy.start()
        w3.append(copy)

    for d in range(co):
        for h in range(last):
            agc.from_inner(h, d)
        backward(agc.from_inner(last, d))

    def back(block, h):
        return acc[rows(block, h, half), :]

    rsr = Reduce(
        remote, "row", rx, rc, ro, ri, back, (rs_y, rr_y, rs_z, rr_z), (sem_ry, sem_rz)
    )
    order = list(range(1, ro)) + [0]
    for h in range(halves):
        for d in order:
            rsr.start(h, d)

    for d in range(1, ncol):
        source = lax.rem(col + d, ncol)
        remote(
            w4.at[row, source], w4.at[row, source], sem_w3.at[0], sem_w3r.at[source], "col", source
        ).wait_recv()
    w4c = []
    for d in range(1, nrow):
        peer = lax.rem(row + d, nrow)
        copy = remote(w4.at[row], w4.at[row], sem_w4.at[d - 1], sem_w4r.at[row], "row", peer)
        copy.start()
        w4c.append(copy)

    for h in range(halves):
        for d in order:
            rsr.middle(h, d)
    for d in range(1, nrow):
        source = lax.rem(row + d, nrow)
        remote(
            w4.at[source], w4.at[source], sem_w4.at[0], sem_w4r.at[source], "row", source
        ).wait_recv()
    for r in range(nrow):
        for k in range(ncol):
            at = r * rows1 + k * rows2
            gw_ref[at : at + rows2, :] = w4[r, k].astype(F32)
    for h in range(halves):
        gin_ref[h * half : (h + 1) * half, :] = lax.dot_general(
            rsr.end(h).astype(BF16), wbuf[...], (((1,), (1,)), ((), ())), preferred_element_type=F32
        ).astype(BF16)
    @pl.when(line.central)
    def _():
        for copy in agc.maybe:
            copy.wait_send()

    for copy in g1.sent + rsc.sent + agc.sent + rsr.sent + w1 + w2 + w3 + w4c:
        copy.wait_send()


def hand_on(a_in, b_in, c_in, a_out, b_out, c_out):
    a_out[...] = a_in[...]
    b_out[...] = b_in[...]
    c_out[...] = c_in[...]


def solution(mesh):
    nrow, ncol = mesh.shape["row"], mesh.shape["col"]
    ro, ri = split_axis(nrow, 2)
    co = 4
    ci = ncol // co
    halves = 2
    dims = (nrow, ncol, ro, ri, co, ci, halves)

    def body(features, weight, grad_out, adj_values, block_pos, block_count):
        own, width = features.shape
        slots, bs, _ = adj_values.shape
        rows_tile = own * ncol
        cols_tile = own * nrow
        spots = (rows_tile // bs) * (cols_tile // bs)
        half = own // halves
        rows1 = width // nrow
        rows2 = rows1 // ncol
        dma = pltpu.SemaphoreType.DMA

        def block(n, rows):
            return pltpu.VMEM((max(n, 1), rows, width), BF16)

        def ag_sends(o, i):
            return max((o - 1) + (i - 1) + (o - 1) * (i - 1), 1)

        scratch = [
            pltpu.VMEM((8, spots), jnp.int32),
            pltpu.SMEM((8, spots), jnp.int32),
            pltpu.VMEM((slots + 1, bs, bs), BF16),
            pltpu.VMEM((rows_tile, cols_tile), BF16),
            pltpu.VMEM((cols_tile, rows_tile), BF16),
            block(nrow, own),
            pltpu.VMEM((width, width), BF16),
            pltpu.VMEM((own, width), BF16),
            block(halves * co * (ci - 1), half),
            block(halves * co * (ci - 1), half),
            block(halves * co, half),
            block(halves * co, half),
            pltpu.VMEM((own, width), BF16),
            block(ncol * halves, half),
            pltpu.VMEM((cols_tile, width), F32),
            block(halves * ro * (ri - 1), half),
            block(halves * ro * (ri - 1), half),
            block(halves * (ro - 1), half),
            block(halves * (ro - 1), half),
            block(nrow, rows1),
            block(nrow - 1, rows1),
            block(ncol, rows2),
            block(ncol - 1, rows2),
            pltpu.VMEM((nrow, ncol, rows2, width), BF16),
            dma((5,)),
            dma((ag_sends(ro, ri),)),
            dma((nrow,)),
            dma((2, max(halves * co * (ci - 1), 1))),
            dma((2, halves * co)),
            dma((halves * (ag_sends(co, ci) + 1),)),
            dma((halves * ncol,)),
            dma((2, max(halves * ro * (ri - 1), 1))),
            dma((2, max(halves * (ro - 1), 1))),
            dma((2, nrow)),
            dma((2, ncol)),
            dma((ncol,)),
            dma((ncol,)),
            dma((nrow,)),
            dma((nrow,)),
        ]
        anyspace = pl.BlockSpec(memory_space=pl.ANY)
        vmem = pl.BlockSpec(memory_space=pltpu.VMEM)
        shapes = (
            jax.ShapeDtypeStruct((own, width), BF16),
            jax.ShapeDtypeStruct((own, width), BF16),
            jax.ShapeDtypeStruct((width, width), F32),
        )
        outs = pl.pallas_call(
            functools.partial(kernel, dims),
            out_shape=shapes,
            in_specs=[pl.BlockSpec(memory_space=pltpu.SMEM), vmem] + [anyspace] * 4,
            out_specs=[vmem] * 3,
            scratch_shapes=scratch,
            compiler_params=pltpu.CompilerParams(
                collective_id=0,
                has_side_effects=True,
                vmem_limit_bytes=66 * 1000 * 1000,
            ),
        )(block_count, block_pos, features, weight, grad_out, adj_values)
        return pl.pallas_call(
            hand_on, out_shape=shapes, in_specs=[vmem] * 3, out_specs=[vmem] * 3
        )(*outs)

    placed = (
        P(("col", "row"), None),
        P(),
        P(("row", "col"), None),
        P("row", "col", None),
        P("row", "col"),
        P("row", "col"),
    )
    return jax.shard_map(
        body,
        mesh=mesh,
        in_specs=placed,
        out_specs=(P(("row", "col"), None), P(("col", "row"), None), P()),
        check_vma=False,
    )
```
